256 devices in a mesh: seq: 128 (over y, x, z), width: 2 (over core).
Axes of the slice: x: 4, y: 4, z: 8, core: 2. Of those that a mesh axis runs over, the one named last changes fastest.
Arguments:
- tokens: bfloat16 [2, 32768, 768], P(None, 'seq', 'width'), may hold values from -6 to 6
- w_in: bfloat16 [768, 3, 768], P(None, None, 'width'), may hold values from -0.21875 to 0.21875
- conv_taps: float32 [3, 3, 768], P(None, None, 'width'), may hold values from -3 to 3
- left_in: bfloat16 [256, 128, 128], P('seq'), may hold values from -0.5 to 0.5
- right_in: bfloat16 [128, 256, 256], P('seq'), may hold values from -0.375 to 0.375
- kernel: bfloat16 [128, 256, 768], P('seq', None, 'width'), may hold values from -6 to 6
- right_out: bfloat16 [128, 256, 256], P('seq'), may hold values from -0.375 to 0.375
- left_out: bfloat16 [256, 128, 128], P('seq'), may hold values from -0.5 to 0.5
- w_out: bfloat16 [768, 768], P('width'), may hold values from -0.21875 to 0.21875
Outputs:
- mixed: bfloat16 [2, 32768, 768], P(None, 'seq', 'width')
The draws below stay inside these ranges and needn't reach their ends.
All inputs are finite; a program needn't handle non-finite values.
Results may differ from the reference program's by a relative error of at most 0.012.
Values may be sent and summed in bfloat16 or wider, within the bound.
A program may use at most 64 MiB of HBM per device.

```python
import jax
import jax.numpy as jnp
from jax import lax

D = 768
A = 256
BATCH = 2
B = 128
LENGTH = 32768


def shard_levels(own_key, extent, pieces, low, top_value):
    loudness = 1.0
    for axis_at, shards_of in pieces:
        steps = jax.random.uniform(jax.random.fold_in(jax.random.fold_in(own_key, 6), axis_at), (shards_of,), jnp.float32, low / len(pieces), top_value / len(pieces))
        loudness = loudness * jnp.repeat(jnp.exp(steps), extent[axis_at] // shards_of).reshape((-1,) + (1,) * (len(extent) - 1 - axis_at))
    return loudness


def centred(stream_key, shape, deviation, reach, shards=(), kind=jnp.bfloat16):
    result = jax.random.normal(stream_key, shape, jnp.float32) * deviation
    if len(shards) > 0:
        result = shard_levels(stream_key, shape, shards, -0.22, 0.18) * result
    return jnp.clip(result, min=-reach, max=reach).astype(kind)


def setup_inputs(seed: int = 0) -> dict:
    seeds = jax.random.split(jax.random.key(seed), 10)
    return {
        "tokens": centred(seeds[0], (BATCH, LENGTH, D), 1.0, 6.0, ((1, 128), (2, 2))),
        "w_in": centred(seeds[1], (D, 3, D), D ** -0.5, 0.21875, ((2, 2),)),
        "conv_taps": centred(seeds[2], (3, 3, D), 0.6, 3.0, ((2, 2),), jnp.float32),
        "left_in": centred(seeds[3], (A, B, B), B ** -0.5, 0.5, ((0, 128),)),
        "right_in": centred(seeds[4], (B, A, A), A ** -0.5, 0.375, ((0, 128),)),
        "kernel": centred(seeds[5], (B, A, D), 1.0, 6.0, ((0, 128), (2, 2))),
        "right_out": centred(seeds[6], (B, A, A), A ** -0.5, 0.375, ((0, 128),)),
        "left_out": centred(seeds[7], (A, B, B), B ** -0.5, 0.5, ((0, 128),)),
        "w_out": centred(seeds[8], (D, D), D ** -0.5, 0.21875, ((0, 2),)),
    }


def one_sequence(tokens_row, w_in, conv_taps, left_in, right_in, kernel, right_out, left_out, w_out):
    width = w_in.shape[0]
    flat = w_in.reshape(width, 3 * width)
    proj = jnp.dot(tokens_row, flat, preferred_element_type=jnp.float32).astype(jnp.bfloat16)
    proj = proj.reshape(LENGTH, 3, width).astype(jnp.float32)
    zero_row = jnp.zeros((1, 3, width), jnp.float32)
    before = jnp.concatenate([zero_row, proj[:-1]], axis=0)
    after = jnp.concatenate([proj[1:], zero_row], axis=0)
    conv = conv_taps[0] * before + conv_taps[1] * proj + conv_taps[2] * after
    gate = conv[:, 0, :]
    u = (conv[:, 1, :] * conv[:, 2, :]).astype(jnp.bfloat16).reshape(A, B, width)
    hp = lax.Precision.HIGHEST
    t1 = jnp.einsum('aib,abc->aic', left_in.astype(jnp.float32), u.astype(jnp.float32), precision=hp).astype(jnp.bfloat16)
    t2 = jnp.einsum('bia,abc->bic', right_in.astype(jnp.float32), t1.astype(jnp.float32), precision=hp)
    freq = (t2 * kernel.astype(jnp.float32)).astype(jnp.bfloat16)
    t3 = jnp.einsum('bia,bac->bic', right_out.astype(jnp.float32), freq.astype(jnp.float32), precision=hp).astype(jnp.bfloat16)
    t4 = jnp.einsum('aib,bac->aic', left_out.astype(jnp.float32), t3.astype(jnp.float32), precision=hp)
    gated = (gate * t4.reshape(LENGTH, width)).astype(jnp.bfloat16)
    return jnp.dot(gated, w_out, preferred_element_type=jnp.float32).astype(jnp.bfloat16)


def reference(tokens, w_in, conv_taps, left_in, right_in, kernel, right_out, left_out, w_out):
    def apply_one(tokens_row):
        return one_sequence(tokens_row, w_in, conv_taps, left_in, right_in, kernel, right_out, left_out, w_out)
    return lax.map(apply_one, tokens)
```

```python
import jax
import jax.numpy as jnp
from jax import lax
from jax.experimental import pallas as pl
from jax.experimental.pallas import tpu as pltpu
from jax.sharding import PartitionSpec as P

BF16 = jnp.bfloat16
F32 = jnp.float32
EDGE = 16
PAD = 8
FIRST = 256


def dot(a, b):
    return jnp.dot(a, b, preferred_element_type=F32)


def spread_rows(count, part):
    rows = lax.broadcasted_iota(jnp.int32, (2 * count, count), 0)
    cols = lax.broadcasted_iota(jnp.int32, (2 * count, count), 1)
    return (rows == 2 * cols + part).astype(BF16)


def spread_cols(count, part):
    rows = lax.broadcasted_iota(jnp.int32, (count, 2 * count), 0)
    cols = lax.broadcasted_iota(jnp.int32, (count, 2 * count), 1)
    return (cols == 2 * rows + part).astype(BF16)


def layer(tok, win, taps, lin, rin, ker, rout, lout, wout, out,
          tokv, wv, tapv, linv, rinv, kerv, routv, loutv, woutv,
          acc, pad, gate, mix_in, mix_out, send1, recv1, send2, recv2, sendt, recvt, outv,
          load_sem, near_send, near_recv, plane_sem, s1, r1, s2, r2, st, rt, out_sem):
    seq = lax.axis_size("seq")
    me = lax.axis_index("seq")
    w = lax.axis_index("width")
    other = 1 - w
    batch, here, half = tok.shape
    lanes = half // 128
    my, mx, mz = me // 32, (me // 8) % 4, me % 8

    def away(k):
        return ((my + k // 32) % 4) * 32 + ((mx + (k // 8) % 4) % 4) * 8 + (mz + k % 8) % 8

    own0 = pl.multiple_of(w * half, half)
    sib0 = pl.multiple_of(other * half, half)
    loads = [
        (tok, tokv.at[:, pl.ds(0, here), pl.ds(0, half)]),
        (win.at[:, pl.ds(own0, half)], wv.at[:, pl.ds(0, half)]),
        (win.at[:, pl.ds(sib0, half)], wv.at[:, pl.ds(half, half)]),
        (taps, tapv),
        (lin, linv),
        (rin, rinv),
        (ker, kerv),
        (rout, routv),
        (lout, loutv),
        (wout.at[:, pl.ds(own0, half)], woutv.at[0]),
        (wout.at[:, pl.ds(sib0, half)], woutv.at[1]),
    ]
    loads = [pltpu.make_async_copy(a, b, load_sem.at[i]) for i, (a, b) in enumerate(loads)]
    for load in loads:
        load.start()

    right, left = (me + 1) % seq, (me + seq - 1) % seq
    barrier = pltpu.get_barrier_semaphore()
    greet = [{"width": other}]
    for s in (right, left):
        greet += [{"seq": s}, {"seq": s, "width": other}]
    greet += [{"seq": away(k)} for k in range(1, 8)]
    greet += [{"seq": away(8 * k)} for k in range(1, 16)]
    for who in greet:
        pl.semaphore_signal(barrier, 1, device_id=who)

    loads[0].wait()
    loads[1].wait()
    for z in range(batch):
        for j in range(3):
            acc[z, j, :here] = dot(tokv[z, :here, 0:FIRST], wv[j, 0:FIRST, :])

    pl.semaphore_wait(barrier, len(greet))
    for k in range(1, 8):
        pl.semaphore_signal(plane_sem, 1, device_id={"seq": away(k)})

    near = []
    mine = tokv.at[:, pl.ds(0, here), pl.ds(0, half)]
    theirs = tokv.at[:, pl.ds(0, here), pl.ds(half, half)]
    near.append((mine, theirs, {"width": other}))
    for s, row, to in ((right, here - EDGE, here), (left, 0, here + EDGE)):
        src = tokv.at[:, pl.ds(row, EDGE), pl.ds(0, half)]
        near.append((src, tokv.at[:, pl.ds(to, EDGE), pl.ds(0, half)], {"seq": s}))
        near.append((src, tokv.at[:, pl.ds(to, EDGE), pl.ds(half, half)], {"seq": s, "width": other}))
    near = [
        pltpu.make_async_remote_copy(a, b, near_send.at[i], near_recv.at[i], device_id=who)
        for i, (a, b, who) in enumerate(near)
    ]
    for copy in near:
        copy.start()

    loads[4].wait()
    loads[8].wait()
    count = linv.shape[1]
    for a in range(2):
        mix_in[:, count * a : count * (a + 1)] = dot(spread_rows(count, a), linv[a]).astype(BF16)
        mix_out[count * a : count * (a + 1), :] = dot(loutv[a], spread_cols(count, a)).astype(BF16)
    loads[2].wait()
    loads[3].wait()
    for copy in near:
        copy.wait_recv()

    edges = jnp.concatenate([tokv[z, here:, 0:FIRST] for z in range(batch)], axis=0)
    for j in range(3):
        part = dot(edges, wv[j, 0:FIRST, :])
        for z in range(batch):
            acc[z, j, here:] = part[2 * EDGE * z : 2 * EDGE * (z + 1)]

    def scatter(src, dst, ssem, rsem, z):
        def step(k, carry):
            d = away(k)
            pltpu.make_async_remote_copy(
                src.at[z, :, d], dst.at[z, :, me], ssem.at[z], rsem.at[z], device_id={"seq": d}
            ).start()
            return carry

        lax.fori_loop(1, seq, step, 0)
        dst[z, :, me] = src[z, :, me]

    def all_of(src, dst, ssem, rsem, z):
        rest = pl.ds(0, seq - 1)
        return pltpu.make_async_remote_copy(
            src.at[z, :, rest], dst.at[z, :, rest], ssem.at[z], rsem.at[z], device_id={"seq": me}
        )

    def put(ref, z, value):
        for l in range(lanes):
            ref[z, l] = value[:, 128 * l : 128 * (l + 1)].reshape(seq, 2, 128)

    def take(ref, z):
        return jnp.concatenate([ref[z, l].reshape(2 * seq, 128) for l in range(lanes)], axis=1)

    first, last = me == 0, me == seq - 1
    for z in range(batch):
        conv = []
        for j in range(3):
            p = acc[z, j] + dot(tokv[z, :, FIRST:], wv[j, FIRST:, :])
            p = p.astype(BF16).astype(F32)
            before = p[here + EDGE - 1 : here + EDGE]
            after = p[here + EDGE : here + EDGE + 1]
            pad[j, PAD - 1 : PAD] = jnp.where(first, 0.0, before)
            pad[j, PAD : PAD + here] = p[:here]
            pad[j, PAD + here : PAD + here + 1] = jnp.where(last, 0.0, after)
            conv.append(
                tapv[0, j : j + 1] * pad[j, PAD - 1 : PAD - 1 + here]
                + tapv[1, j : j + 1] * pad[j, PAD : PAD + here]
                + tapv[2, j : j + 1] * pad[j, PAD + 1 : PAD + 1 + here]
            )
            if j == 0:
                gate[z] = conv[0]
        u = (conv[1] * conv[2]).astype(BF16)
        put(send1, z, dot(mix_in[...], u).astype(BF16))
        if z == 0:
            pl.semaphore_wait(plane_sem, 7)
        scatter(send1, recv1, s1, r1, z)

    loads[5].wait()
    loads[6].wait()
    loads[7].wait()
    for z in range(batch):
        all_of(send1, recv1, s1, r1, z).wait_recv()
        second = dot(rinv[...], take(recv1, z))
        freq = (second * kerv[...].astype(F32)).astype(BF16)
        put(send2, z, dot(routv[...], freq).astype(BF16))
        scatter(send2, recv2, s2, r2, z)

    loads[9].wait()
    loads[10].wait()
    shares, writes = [], []
    for z in range(batch):
        all_of(send2, recv2, s2, r2, z).wait_recv()
        fourth = dot(mix_out[...], take(recv2, z))
        y = (gate[z] * fourth).astype(BF16)
        sendt[z] = dot(y, woutv[1]).astype(BF16)
        share = pltpu.make_async_remote_copy(
            sendt.at[z], recvt.at[z], st.at[z], rt.at[z], device_id={"width": other}
        )
        share.start()
        own = dot(y, woutv[0])
        share.wait_recv()
        outv[z] = (own + recvt[z].astype(F32)).astype(BF16)
        write = pltpu.make_async_copy(outv.at[z], out.at[z], out_sem.at[z])
        write.start()
        shares.append(share)
        writes.append(write)

    for copy in near + shares:
        copy.wait_send()
    for z in range(batch):
        all_of(send1, recv1, s1, r1, z).wait_send()
        all_of(send2, recv2, s2, r2, z).wait_send()
    for write in writes:
        write.wait()


def shards(tokens, w_in, conv_taps, left_in, right_in, kernel, right_out, left_out, w_out):
    batch, here, half = tokens.shape
    width = w_in.shape[0]
    seq = lax.axis_size("seq")
    lanes = half // 128
    rows = here + 2 * EDGE
    any_space = pl.BlockSpec(memory_space=pltpu.HBM)
    dma, regular = pltpu.SemaphoreType.DMA, pltpu.SemaphoreType.REGULAR
    exchange = pltpu.VMEM((batch, lanes, seq, 2, 128), BF16)
    args = (tokens, w_in.transpose(1, 0, 2), conv_taps, left_in, right_in[0], kernel[0], right_out[0], left_out, w_out)
    return pl.pallas_call(
        layer,
        out_shape=jax.ShapeDtypeStruct((batch, here, half), BF16),
        in_specs=[any_space] * len(args),
        out_specs=any_space,
        scratch_shapes=[
            pltpu.VMEM((batch, rows, width), BF16),
            pltpu.VMEM((3, width, half), BF16),
            pltpu.VMEM(conv_taps.shape, F32),
            pltpu.VMEM(left_in.shape, BF16),
            pltpu.VMEM(right_in.shape[1:], BF16),
            pltpu.VMEM(kernel.shape[1:], BF16),
            pltpu.VMEM(right_out.shape[1:], BF16),
            pltpu.VMEM(left_out.shape, BF16),
            pltpu.VMEM((2, half, half), BF16),
            pltpu.VMEM((batch, 3, rows, half), F32),
            pltpu.VMEM((3, here + 2 * PAD, half), F32),
            pltpu.VMEM((batch, here, half), F32),
            pltpu.VMEM((here, here), BF16),
            pltpu.VMEM((here, here), BF16),
            exchange, exchange, exchange, exchange,
            pltpu.VMEM((batch, here, half), BF16),
            pltpu.VMEM((batch, here, half), BF16),
            pltpu.VMEM((batch, here, half), BF16),
            dma((11,)), dma((5,)), dma((5,)), regular,
            dma((batch,)), dma((batch,)), dma((batch,)), dma((batch,)),
            dma((batch,)), dma((batch,)), dma((batch,)),
        ],
        compiler_params=pltpu.CompilerParams(collective_id=0, has_side_effects=True, vmem_limit_bytes=60000 * 1024),
        name="monarch_layer",
    )(*args)


def solution(mesh):
    in_specs = (
        P(None, "seq", "width"),
        P(None, None, "width"),
        P(None, None, "width"),
        P("seq", None, None),
        P("seq", None, None),
        P("seq", None, "width"),
        P("seq", None, None),
        P("seq", None, None),
        P("width", None),
    )
    out_specs = P(None, "seq", "width")
    return jax.shard_map(shards, mesh=mesh, in_specs=in_specs, out_specs=out_specs, check_vma=False)
```

```python
import jax
import jax.numpy as jnp
from jax import lax
from jax.experimental import pallas as pl
from jax.experimental.pallas import tpu as pltpu
from jax.sharding import PartitionSpec as P

BF16 = jnp.bfloat16
F32 = jnp.float32
EDGE = 16
PAD = 8
FIRST = 256


def dot(a, b):
    return jnp.dot(a, b, preferred_element_type=F32)


def spread_rows(count, part):
    rows = lax.broadcasted_iota(jnp.int32, (2 * count, count), 0)
    cols = lax.broadcasted_iota(jnp.int32, (2 * count, count), 1)
    return (rows == 2 * cols + part).astype(BF16)


def spread_cols(count, part):
    rows = lax.broadcasted_iota(jnp.int32, (count, 2 * count), 0)
    cols = lax.broadcasted_iota(jnp.int32, (count, 2 * count), 1)
    return (cols == 2 * rows + part).astype(BF16)


def layer(tok, win, taps, lin, rin, ker, rout, lout, wout, out, recvt,
          tokv, wv, tapv, linv, rinv, kerv, routv, loutv, woutv,
          acc, pad, gate, mix_in, mix_out, send1, recv1, send2, recv2, sendt,
          load_sem, near_send, near_recv, plane_sem, s1, r1, s2, r2, st, rt):
    seq = lax.axis_size("seq")
    me = lax.axis_index("seq")
    w = lax.axis_index("width")
    other = 1 - w
    batch, here, half = tok.shape
    lanes = half // 128
    my, mx, mz = me // 32, (me // 8) % 4, me % 8

    ys = [((my + i) % 4) * 32 for i in range(4)]
    xs = [((mx + i) % 4) * 8 for i in range(4)]
    zs = [(mz + i) % 8 for i in range(8)]

    def away(k):
        return ys[k // 32] + xs[(k // 8) % 4] + zs[k % 8]

    own0 = pl.multiple_of(w * half, half)
    sib0 = pl.multiple_of(other * half, half)
    loads = [
        (tok, tokv.at[:, pl.ds(0, here), pl.ds(0, half)]),
        (win.at[:, pl.ds(own0, half)], wv.at[:, pl.ds(0, half)]),
        (win.at[:, pl.ds(sib0, half)], wv.at[:, pl.ds(half, half)]),
        (taps, tapv),
        (lin, linv),
        (rin, rinv),
        (ker, kerv),
        (rout, routv),
        (lout, loutv),
        (wout.at[:, pl.ds(own0, half)], woutv.at[0]),
        (wout.at[:, pl.ds(sib0, half)], woutv.at[1]),
    ]
    loads = [pltpu.make_async_copy(a, b, load_sem.at[i]) for i, (a, b) in enumerate(loads)]
    for load in loads:
        load.start()

    right, left = (me + 1) % seq, (me + seq - 1) % seq
    barrier = pltpu.get_barrier_semaphore()
    greet = [{"width": other}]
    for s in (right, left):
        greet += [{"seq": s}, {"seq": s, "width": other}]
    greet += [{"seq": away(k)} for k in range(1, 8)]
    greet += [{"seq": away(8 * k)} for k in range(1, 16)]
    for who in greet:
        pl.semaphore_signal(barrier, 1, device_id=who)

    pl.semaphore_wait(barrier, len(greet))
    loads[0].wait()
    near = []
    near.append((tokv.at[:, pl.ds(0, here), pl.ds(0, half)], tokv.at[:, pl.ds(0, here), pl.ds(half, half)], {"width": other}))
    for s, row, to in ((right, here - EDGE, here), (left, 0, here + EDGE)):
        src = tokv.at[:, pl.ds(row, EDGE), pl.ds(0, half)]
        near.append((src, tokv.at[:, pl.ds(to, EDGE), pl.ds(0, half)], {"seq": s}))
        near.append((src, tokv.at[:, pl.ds(to, EDGE), pl.ds(half, half)], {"seq": s, "width": other}))
    near = [
        pltpu.make_async_remote_copy(a, b, near_send.at[i], near_recv.at[i], device_id=who)
        for i, (a, b, who) in enumerate(near)
    ]
    for copy in near:
        copy.start()
    for k in range(1, 8):
        pl.semaphore_signal(plane_sem, 1, device_id={"seq": away(k)})

    loads[1].wait()
    for z in range(batch):
        for j in range(3):
            acc[z, j, :here] = dot(tokv[z, :here, 0:FIRST], wv[j, 0:FIRST, :])

    loads[4].wait()
    loads[8].wait()
    count = linv.shape[1]
    for a in range(2):
        mix_in[:, count * a : count * (a + 1)] = dot(spread_rows(count, a), linv[a]).astype(BF16)
        mix_out[count * a : count * (a + 1), :] = dot(loutv[a], spread_cols(count, a)).astype(BF16)
    loads[2].wait()
    loads[3].wait()
    for copy in near:
        copy.wait_recv()

    edges = jnp.concatenate([tokv[z, here:, 0:FIRST] for z in range(batch)], axis=0)
    for j in range(3):
        part = dot(edges, wv[j, 0:FIRST, :])
        for z in range(batch):
            acc[z, j, here:] = part[2 * EDGE * z : 2 * EDGE * (z + 1)]

    def hops(k):
        return sum(min(i, n - i) for i, n in ((k // 32, 4), (k // 8 % 4, 4), (k % 8, 8)))

    order = sorted(range(1, seq), key=hops, reverse=True)

    def scatter(src, dst, ssem, rsem, z):
        for k in order:
            d = away(k)
            pltpu.make_async_remote_copy(
                src.at[z, :, d], dst.at[z, :, me], ssem.at[z], rsem.at[z], device_id={"seq": d}
            ).start()
        dst[z, :, me] = src[z, :, me]

    def all_of(src, dst, ssem, rsem, z):
        rest = pl.ds(0, seq - 1)
        return pltpu.make_async_remote_copy(
            src.at[z, :, rest], dst.at[z, :, rest], ssem.at[z], rsem.at[z], device_id={"seq": me}
        )

    def put(ref, z, value):
        for l in range(lanes):
            ref[z, l] = value[:, 128 * l : 128 * (l + 1)].reshape(seq, 2, 128)

    def take(ref, z):
        return jnp.concatenate([ref[z, l].reshape(2 * seq, 128) for l in range(lanes)], axis=1)

    first, last = me == 0, me == seq - 1
    for z in range(batch):
        conv = []
        for j in range(3):
            p = acc[z, j] + dot(tokv[z, :, FIRST:], wv[j, FIRST:, :])
            p = p.astype(BF16).astype(F32)
            before = p[here + EDGE - 1 : here + EDGE]
            after = p[here + EDGE : here + EDGE + 1]
            pad[j, PAD - 1 : PAD] = jnp.where(first, 0.0, before)
            pad[j, PAD : PAD + here] = p[:here]
            pad[j, PAD + here : PAD + here + 1] = jnp.where(last, 0.0, after)
            conv.append(
                tapv[0, j : j + 1] * pad[j, PAD - 1 : PAD - 1 + here]
                + tapv[1, j : j + 1] * pad[j, PAD : PAD + here]
                + tapv[2, j : j + 1] * pad[j, PAD + 1 : PAD + 1 + here]
            )
            if j == 0:
                gate[z] = conv[0]
        u = (conv[1] * conv[2]).astype(BF16)
        put(send1, z, dot(mix_in[...], u).astype(BF16))
        if z == 0:
            pl.semaphore_wait(plane_sem, 7)
        scatter(send1, recv1, s1, r1, z)

    loads[5].wait()
    loads[6].wait()
    loads[7].wait()
    for z in range(batch):
        all_of(send1, recv1, s1, r1, z).wait_recv()
        second = dot(rinv[...], take(recv1, z))
        freq = (second * kerv[...].astype(F32)).astype(BF16)
        put(send2, z, dot(routv[...], freq).astype(BF16))
        scatter(send2, recv2, s2, r2, z)

    loads[9].wait()
    loads[10].wait()
    shares = []
    for z in range(batch):
        all_of(send2, recv2, s2, r2, z).wait_recv()
        fourth = dot(mix_out[...], take(recv2, z))
        y = (gate[z] * fourth).astype(BF16)
        sendt[z] = dot(y, woutv[1]).astype(BF16)
        share = pltpu.make_async_remote_copy(
            sendt.at[z], recvt.at[z], st.at[z], rt.at[z], device_id={"width": other}
        )
        share.start()
        own = dot(y, woutv[0])
        share.wait_recv()
        out[z] = own.astype(BF16)
        shares.append(share)

    for copy in near + shares:
        copy.wait_send()
    for z in range(batch):
        all_of(send1, recv1, s1, r1, z).wait_send()
        all_of(send2, recv2, s2, r2, z).wait_send()


def shards(tokens, w_in, conv_taps, left_in, right_in, kernel, right_out, left_out, w_out):
    batch, here, half = tokens.shape
    width = w_in.shape[0]
    seq = lax.axis_size("seq")
    lanes = half // 128
    rows = here + 2 * EDGE
    any_space = pl.BlockSpec(memory_space=pltpu.HBM)
    dma, regular = pltpu.SemaphoreType.DMA, pltpu.SemaphoreType.REGULAR
    exchange = pltpu.VMEM((batch, lanes, seq, 2, 128), BF16)
    args = (tokens, w_in.transpose(1, 0, 2), conv_taps, left_in, right_in[0], kernel[0], right_out[0], left_out, w_out)
    args = tuple(pltpu.with_memory_space_constraint(a, pltpu.HBM) for a in args)
    own, theirs = pl.pallas_call(
        layer,
        out_shape=[jax.ShapeDtypeStruct((batch, here, half), BF16)] * 2,
        in_specs=[any_space] * len(args),
        out_specs=[pl.BlockSpec(memory_space=pltpu.VMEM)] * 2,
        scratch_shapes=[
            pltpu.VMEM((batch, rows, width), BF16),
            pltpu.VMEM((3, width, half), BF16),
            pltpu.VMEM(conv_taps.shape, F32),
            pltpu.VMEM(left_in.shape, BF16),
            pltpu.VMEM(right_in.shape[1:], BF16),
            pltpu.VMEM(kernel.shape[1:], BF16),
            pltpu.VMEM(right_out.shape[1:], BF16),
            pltpu.VMEM(left_out.shape, BF16),
            pltpu.VMEM((2, half, half), BF16),
            pltpu.VMEM((batch, 3, rows, half), F32),
            pltpu.VMEM((3, here + 2 * PAD, half), F32),
            pltpu.VMEM((batch, here, half), F32),
            pltpu.VMEM((here, here), BF16),
            pltpu.VMEM((here, here), BF16),
            exchange, exchange, exchange, exchange,
            pltpu.VMEM((batch, here, half), BF16),
            dma((11,)), dma((5,)), dma((5,)), regular,
            dma((batch,)), dma((batch,)), dma((batch,)), dma((batch,)),
            dma((batch,)), dma((batch,)),
        ],
        compiler_params=pltpu.CompilerParams(collective_id=0, has_side_effects=True, vmem_limit_bytes=24 * 1024 * 1024),
        name="monarch_layer",
    )(*args)
    return (own.astype(F32) + theirs.astype(F32)).astype(BF16)


def solution(mesh):
    in_specs = (
        P(None, "seq", "width"),
        P(None, None, "width"),
        P(None, None, "width"),
        P("seq", None, None),
        P("seq", None, None),
        P("seq", None, "width"),
        P("seq", None, None),
        P("seq", None, None),
        P("width", None),
    )
    out_specs = P(None, "seq", "width")
    return jax.shard_map(shards, mesh=mesh, in_specs=in_specs, out_specs=out_specs, check_vma=False)
```

```python
import jax
import jax.numpy as jnp
from jax import lax
from jax.experimental import pallas as pl
from jax.experimental.pallas import tpu as pltpu
from jax.sharding import PartitionSpec as P

BF16 = jnp.bfloat16
F32 = jnp.float32
EDGE = 16
PAD = 8
FIRST = 256


def dot(a, b):
    return jnp.dot(a, b, preferred_element_type=F32)


def spread_rows(count, part):
    rows = lax.broadcasted_iota(jnp.int32, (2 * count, count), 0)
    cols = lax.broadcasted_iota(jnp.int32, (2 * count, count), 1)
    return (rows == 2 * cols + part).astype(BF16)


def spread_cols(count, part):
    rows = lax.broadcasted_iota(jnp.int32, (count, 2 * count), 0)
    cols = lax.broadcasted_iota(jnp.int32, (count, 2 * count), 1)
    return (cols == 2 * rows + part).astype(BF16)


def layer(tok, win, taps, lin, rin, ker, rout, lout, wout, out, recvt,
          tokv, wv, tapv, linv, rinv, kerv, routv, loutv, woutv,
          acc, pad, gate, mix_in, mix_out, send1, recv1, send2, recv2, sendt,
          load_sem, near_send, near_recv, plane_sem, s1, r1, s2, r2, st, rt):
    seq = lax.axis_size("seq")
    me = lax.axis_index("seq")
    w = lax.axis_index("width")
    other = 1 - w
    batch, here, half = tok.shape
    lanes = half // 128
    my, mx, mz = me // 32, (me // 8) % 4, me % 8

    turn = 1 - 2 * w
    ys = [((my + 4 + turn * i) % 4) * 32 for i in range(4)]
    xs = [((mx + 4 + turn * i) % 4) * 8 for i in range(4)]
    zs = [(mz + 8 + turn * i) % 8 for i in range(8)]

    def away(k):
        return ys[k // 32] + xs[(k // 8) % 4] + zs[k % 8]

    own0 = pl.multiple_of(w * half, half)
    sib0 = pl.multiple_of(other * half, half)
    loads = [
        (tok, tokv.at[:, pl.ds(0, here), pl.ds(0, half)]),
        (win.at[:, pl.ds(own0, half)], wv.at[:, pl.ds(0, half)]),
        (win.at[:, pl.ds(sib0, half)], wv.at[:, pl.ds(half, half)]),
        (taps, tapv),
        (lin, linv),
        (rin, rinv),
        (ker, kerv),
        (rout, routv),
        (lout, loutv),
        (wout.at[:, pl.ds(own0, half)], woutv.at[0]),
        (wout.at[:, pl.ds(sib0, half)], woutv.at[1]),
    ]
    loads = [pltpu.make_async_copy(a, b, load_sem.at[i]) for i, (a, b) in enumerate(loads)]
    for load in loads:
        load.start()

    right, left = (me + 1) % seq, (me + seq - 1) % seq
    barrier = pltpu.get_barrier_semaphore()
    greet = [{"width": other}]
    for s in (right, left):
        greet += [{"seq": s}, {"seq": s, "width": other}]
    greet += [{"seq": away(k)} for k in range(1, 8)]
    greet += [{"seq": away(8 * k)} for k in range(1, 16)]
    for who in greet:
        pl.semaphore_signal(barrier, 1, device_id=who)

    pl.semaphore_wait(barrier, len(greet))
    loads[0].wait()
    near = []
    near.append((tokv.at[:, pl.ds(0, here), pl.ds(0, half)], tokv.at[:, pl.ds(0, here), pl.ds(half, half)], {"width": other}))
    for s, row, to in ((right, here - EDGE, here), (left, 0, here + EDGE)):
        src = tokv.at[:, pl.ds(row, EDGE), pl.ds(0, half)]
        near.append((src, tokv.at[:, pl.ds(to, EDGE), pl.ds(0, half)], {"seq": s}))
        near.append((src, tokv.at[:, pl.ds(to, EDGE), pl.ds(half, half)], {"seq": s, "width": other}))
    near = [
        pltpu.make_async_remote_copy(a, b, near_send.at[i], near_recv.at[i], device_id=who)
        for i, (a, b, who) in enumerate(near)
    ]
    for copy in near:
        copy.start()
    for k in range(1, 8):
        pl.semaphore_signal(plane_sem, 1, device_id={"seq": away(k)})

    loads[1].wait()
    for z in range(batch):
        for j in range(3):
            acc[z, j, :here] = dot(tokv[z, :here, 0:FIRST], wv[j, 0:FIRST, :])

    loads[4].wait()
    loads[8].wait()
    count = linv.shape[1]
    for a in range(2):
        mix_in[:, count * a : count * (a + 1)] = dot(spread_rows(count, a), linv[a]).astype(BF16)
        mix_out[count * a : count * (a + 1), :] = dot(loutv[a], spread_cols(count, a)).astype(BF16)
    loads[2].wait()
    loads[3].wait()
    for copy in near:
        copy.wait_recv()

    edges = jnp.concatenate([tokv[z, here:, 0:FIRST] for z in range(batch)], axis=0)
    for j in range(3):
        part = dot(edges, wv[j, 0:FIRST, :])
        for z in range(batch):
            acc[z, j, here:] = part[2 * EDGE * z : 2 * EDGE * (z + 1)]

    def hops(k):
        return sum(min(i, n - i) for i, n in ((k // 32, 4), (k // 8 % 4, 4), (k % 8, 8)))

    order = sorted(range(1, seq), key=hops, reverse=True)

    def scatter(src, dst, ssem, rsem, z, early=False):
        head = jnp.where(me == 0, away(order[0]), 0)
        for k in order:
            d = away(k)
            if early:
                d = head if k == order[0] else jnp.where(d == 0, away(order[0]), d)
            pltpu.make_async_remote_copy(
                src.at[z, :, d], dst.at[z, :, me], ssem.at[z], rsem.at[z], device_id={"seq": d}
            ).start()
        dst[z, :, me] = src[z, :, me]

    def all_of(src, dst, ssem, rsem, z):
        rest = pl.ds(0, seq - 1)
        return pltpu.make_async_remote_copy(
            src.at[z, :, rest], dst.at[z, :, rest], ssem.at[z], rsem.at[z], device_id={"seq": me}
        )

    def put(ref, z, value):
        for l in range(lanes):
            ref[z, l] = value[:, 128 * l : 128 * (l + 1)].reshape(seq, 2, 128)

    def take(ref, z):
        return jnp.concatenate([ref[z, l].reshape(2 * seq, 128) for l in range(lanes)], axis=1)

    first, last = me == 0, me == seq - 1
    for z in range(batch):
        conv = []
        for j in range(3):
            p = acc[z, j] + dot(tokv[z, :, FIRST:], wv[j, FIRST:, :])
            p = p.astype(BF16).astype(F32)
            before = p[here + EDGE - 1 : here + EDGE]
            after = p[here + EDGE : here + EDGE + 1]
            pad[j, PAD - 1 : PAD] = jnp.where(first, 0.0, before)
            pad[j, PAD : PAD + here] = p[:here]
            pad[j, PAD + here : PAD + here + 1] = jnp.where(last, 0.0, after)
            conv.append(
                tapv[0, j : j + 1] * pad[j, PAD - 1 : PAD - 1 + here]
                + tapv[1, j : j + 1] * pad[j, PAD : PAD + here]
                + tapv[2, j : j + 1] * pad[j, PAD + 1 : PAD + 1 + here]
            )
            if j == 0:
                gate[z] = conv[0]
        u = (conv[1] * conv[2]).astype(BF16)
        put(send1, z, dot(mix_in[...], u).astype(BF16))
        if z == 0:
            pl.semaphore_wait(plane_sem, 7)
        scatter(send1, recv1, s1, r1, z)

    loads[5].wait()
    loads[6].wait()
    loads[7].wait()
    for z in range(batch):
        all_of(send1, recv1, s1, r1, z).wait_recv()
        second = dot(rinv[...], take(recv1, z))
        freq = (second * kerv[...].astype(F32)).astype(BF16)
        put(send2, z, dot(routv[...], freq).astype(BF16))
        scatter(send2, recv2, s2, r2, z, z == 1)

    loads[9].wait()
    loads[10].wait()
    for copy in near:
        copy.wait_send()
    for z in range(batch):
        all_of(send1, recv1, s1, r1, z).wait_send()
    shares = []
    for z in range(batch):
        all_of(send2, recv2, s2, r2, z).wait_recv()
        fourth = dot(mix_out[...], take(recv2, z))
        y = (gate[z] * fourth).astype(BF16)
        sendt[z] = dot(y, woutv[1]).astype(BF16)
        share = pltpu.make_async_remote_copy(
            sendt.at[z], recvt.at[z], st.at[z], rt.at[z], device_id={"width": other}
        )
        share.start()
        own = dot(y, woutv[0])
        out[z] = own.astype(BF16)
        shares.append(share)

    for z in range(batch):
        all_of(send2, recv2, s2, r2, z).wait_send()
    for share in shares:
        share.wait()


def shards(tokens, w_in, conv_taps, left_in, right_in, kernel, right_out, left_out, w_out):
    batch, here, half = tokens.shape
    width = w_in.shape[0]
    seq = lax.axis_size("seq")
    lanes = half // 128
    rows = here + 2 * EDGE
    any_space = pl.BlockSpec(memory_space=pltpu.HBM)
    dma, regular = pltpu.SemaphoreType.DMA, pltpu.SemaphoreType.REGULAR
    exchange = pltpu.VMEM((batch, lanes, seq, 2, 128), BF16)
    args = (tokens, w_in.transpose(1, 0, 2), conv_taps, left_in, right_in[0], kernel[0], right_out[0], left_out, w_out)
    args = tuple(pltpu.with_memory_space_constraint(a, pltpu.HBM) for a in args)
    own, theirs = pl.pallas_call(
        layer,
        out_shape=[jax.ShapeDtypeStruct((batch, here, half), BF16)] * 2,
        in_specs=[any_space] * len(args),
        out_specs=[pl.BlockSpec(memory_space=pltpu.VMEM)] * 2,
        scratch_shapes=[
            pltpu.VMEM((batch, rows, width), BF16),
            pltpu.VMEM((3, width, half), BF16),
            pltpu.VMEM(conv_taps.shape, F32),
            pltpu.VMEM(left_in.shape, BF16),
            pltpu.VMEM(right_in.shape[1:], BF16),
            pltpu.VMEM(kernel.shape[1:], BF16),
            pltpu.VMEM(right_out.shape[1:], BF16),
            pltpu.VMEM(left_out.shape, BF16),
            pltpu.VMEM((2, half, half), BF16),
            pltpu.VMEM((batch, 3, rows, half), F32),
            pltpu.VMEM((3, here + 2 * PAD, half), F32),
            pltpu.VMEM((batch, here, half), F32),
            pltpu.VMEM((here, here), BF16),
            pltpu.VMEM((here, here), BF16),
            exchange, exchange, exchange, exchange,
            pltpu.VMEM((batch, here, half), BF16),
            dma((11,)), dma((5,)), dma((5,)), regular,
            dma((batch,)), dma((batch,)), dma((batch,)), dma((batch,)),
            dma((batch,)), dma((batch,)),
        ],
        compiler_params=pltpu.CompilerParams(collective_id=0, has_side_effects=True, vmem_limit_bytes=24 * 1024 * 1024),
        name="monarch_layer",
    )(*args)
    return (own.astype(F32) + theirs.astype(F32)).astype(BF16)


def solution(mesh):
    in_specs = (
        P(None, "seq", "width"),
        P(None, None, "width"),
        P(None, None, "width"),
        P("seq", None, None),
        P("seq", None, None),
        P("seq", None, "width"),
        P("seq", None, None),
        P("seq", None, None),
        P("width", None),
    )
    out_specs = P(None, "seq", "width")
    return jax.shard_map(shards, mesh=mesh, in_specs=in_specs, out_specs=out_specs, check_vma=False)
```

```python
import jax
import jax.numpy as jnp
from jax import lax
from jax.experimental import pallas as pl
from jax.experimental.pallas import tpu as pltpu
from jax.sharding import PartitionSpec as P

BF16 = jnp.bfloat16
F32 = jnp.float32
EDGE = 16
PAD = 8
FIRST = 256


def dot(a, b):
    return jnp.dot(a, b, preferred_element_type=F32)


def spread_rows(count, part):
    rows = lax.broadcasted_iota(jnp.int32, (2 * count, count), 0)
    cols = lax.broadcasted_iota(jnp.int32, (2 * count, count), 1)
    return (rows == 2 * cols + part).astype(BF16)


def spread_cols(count, part):
    rows = lax.broadcasted_iota(jnp.int32, (count, 2 * count), 0)
    cols = lax.broadcasted_iota(jnp.int32, (count, 2 * count), 1)
    return (cols == 2 * rows + part).astype(BF16)


def layer(tok, win, taps, lin, rin, ker, rout, lout, wout, out, recvt,
          tokv, wv, tapv, linv, rinv, kerv, routv, loutv, woutv,
          acc, rim, pad, gate, mix_in, mix_out, send1, recv1, send2, recv2, sendt,
          load_sem, near_send, near_recv, plane_sem, s1, r1, s2, r2, st, rt):
    seq = lax.axis_size("seq")
    me = lax.axis_index("seq")
    w = lax.axis_index("width")
    other = 1 - w
    batch, here, half = tok.shape
    lanes = half // 128
    my, mx, mz = me // 32, (me // 8) % 4, me % 8

    turn = 1 - 2 * w
    ys = [((my + 4 + turn * i) % 4) * 32 for i in range(4)]
    xs = [((mx + 4 + turn * i) % 4) * 8 for i in range(4)]
    zs = [(mz + 8 + turn * i) % 8 for i in range(8)]

    def away(k):
        return ys[k // 32] + xs[(k // 8) % 4] + zs[k % 8]

    own0 = pl.multiple_of(w * half, half)
    sib0 = pl.multiple_of(other * half, half)
    loads = [
        (tok, tokv.at[:, pl.ds(0, here), pl.ds(0, half)]),
        (win.at[:, pl.ds(own0, half)], wv.at[:, pl.ds(0, half)]),
        (win.at[:, pl.ds(sib0, half)], wv.at[:, pl.ds(half, half)]),
        (taps, tapv),
        (lin, linv),
        (rin, rinv),
        (ker, kerv),
        (rout, routv),
        (lout, loutv),
        (wout.at[:, pl.ds(own0, half)], woutv.at[0]),
        (wout.at[:, pl.ds(sib0, half)], woutv.at[1]),
    ]
    loads = [pltpu.make_async_copy(a, b, load_sem.at[i]) for i, (a, b) in enumerate(loads)]
    for load in loads:
        load.start()

    right, left = (me + 1) % seq, (me + seq - 1) % seq
    barrier = pltpu.get_barrier_semaphore()
    greet = [{"width": other}]
    for s in (right, left):
        greet += [{"seq": s}, {"seq": s, "width": other}]
    greet += [{"seq": away(k)} for k in range(1, 8)]
    greet += [{"seq": away(8 * k)} for k in range(1, 16)]
    for who in greet:
        pl.semaphore_signal(barrier, 1, device_id=who)

    pl.semaphore_wait(barrier, len(greet))
    loads[0].wait()
    near = []
    near.append((tokv.at[:, pl.ds(0, here), pl.ds(0, half)], tokv.at[:, pl.ds(0, here), pl.ds(half, half)], {"width": other}))
    for s, row, to in ((right, here - EDGE, here), (left, 0, here + EDGE)):
        src = tokv.at[:, pl.ds(row, EDGE), pl.ds(0, half)]
        near.append((src, tokv.at[:, pl.ds(to, EDGE), pl.ds(0, half)], {"seq": s}))
        near.append((src, tokv.at[:, pl.ds(to, EDGE), pl.ds(half, half)], {"seq": s, "width": other}))
    near = [
        pltpu.make_async_remote_copy(a, b, near_send.at[i], near_recv.at[i], device_id=who)
        for i, (a, b, who) in enumerate(near)
    ]
    for copy in near[1:] + near[:1]:
        copy.start()
    for k in range(1, 8):
        pl.semaphore_signal(plane_sem, 1, device_id={"seq": away(k)})

    loads[1].wait()
    for z in range(batch):
        for j in range(3):
            acc[z, j] = dot(tokv[z, :here, 0:FIRST], wv[j, 0:FIRST, :])

    loads[4].wait()
    loads[8].wait()
    count = linv.shape[1]
    for a in range(2):
        mix_in[:, count * a : count * (a + 1)] = dot(spread_rows(count, a), linv[a]).astype(BF16)
        mix_out[count * a : count * (a + 1), :] = dot(loutv[a], spread_cols(count, a)).astype(BF16)
    loads[2].wait()
    loads[3].wait()
    def rest(z):
        for j in range(3):
            whole = acc[z, j] + dot(tokv[z, :here, FIRST:], wv[j, FIRST:, :])
            pad[z, j, PAD : PAD + here] = whole.astype(BF16).astype(F32)

    near[0].wait_recv()
    for z in range(batch):
        rest(z)
    for copy in near[1:]:
        copy.wait_recv()
    edges = jnp.concatenate([tokv[z, here:, :] for z in range(batch)], axis=0)
    for j in range(3):
        rim[j] = dot(edges, wv[j]).astype(BF16).astype(F32)

    def hops(k):
        return sum(min(i, n - i) for i, n in ((k // 32, 4), (k // 8 % 4, 4), (k % 8, 8)))

    order = sorted(range(1, seq), key=hops, reverse=True)

    def scatter(src, dst, ssem, rsem, z, early=False):
        head = jnp.where(me == 0, away(order[0]), 0)
        for k in order:
            d = away(k)
            if early:
                d = head if k == order[0] else jnp.where(d == 0, away(order[0]), d)
            pltpu.make_async_remote_copy(
                src.at[z, :, d], dst.at[z, :, me], ssem.at[z], rsem.at[z], device_id={"seq": d}
            ).start()
        dst[z, :, me] = src[z, :, me]

    def all_of(src, dst, ssem, rsem, z):
        rest = pl.ds(0, seq - 1)
        return pltpu.make_async_remote_copy(
            src.at[z, :, rest], dst.at[z, :, rest], ssem.at[z], rsem.at[z], device_id={"seq": me}
        )

    def put(ref, z, value):
        for l in range(lanes):
            ref[z, l] = value[:, 128 * l : 128 * (l + 1)].reshape(seq, 2, 128)

    def take(ref, z):
        return jnp.concatenate([ref[z, l].reshape(2 * seq, 128) for l in range(lanes)], axis=1)

    first, last = me == 0, me == seq - 1
    for z in range(batch):
        conv = []
        for j in range(3):
            low = 2 * EDGE * z + EDGE - 1
            pad[z, j, PAD - 1 : PAD] = jnp.where(first, 0.0, rim[j, low : low + 1])
            pad[z, j, PAD + here : PAD + here + 1] = jnp.where(last, 0.0, rim[j, low + 1 : low + 2])
            conv.append(
                tapv[0, j : j + 1] * pad[z, j, PAD - 1 : PAD - 1 + here]
                + tapv[1, j : j + 1] * pad[z, j, PAD : PAD + here]
                + tapv[2, j : j + 1] * pad[z, j, PAD + 1 : PAD + 1 + here]
            )
            if j == 0:
                gate[z] = conv[0]
        u = (conv[1] * conv[2]).astype(BF16)
        put(send1, z, dot(mix_in[...], u).astype(BF16))
        if z == 0:
            pl.semaphore_wait(plane_sem, 7)
        scatter(send1, recv1, s1, r1, z)

    loads[5].wait()
    loads[6].wait()
    loads[7].wait()
    for z in range(batch):
        all_of(send1, recv1, s1, r1, z).wait_recv()
        second = dot(rinv[...], take(recv1, z))
        freq = (second * kerv[...].astype(F32)).astype(BF16)
        put(send2, z, dot(routv[...], freq).astype(BF16))
        scatter(send2, recv2, s2, r2, z, z == 1)

    loads[9].wait()
    loads[10].wait()
    for copy in near:
        copy.wait_send()
    for z in range(batch):
        all_of(send1, recv1, s1, r1, z).wait_send()
    shares = []
    for z in range(batch):
        all_of(send2, recv2, s2, r2, z).wait_recv()
        fourth = dot(mix_out[...], take(recv2, z))
        y = (gate[z] * fourth).astype(BF16)
        sendt[z] = dot(y, woutv[1]).astype(BF16)
        share = pltpu.make_async_remote_copy(
            sendt.at[z], recvt.at[z], st.at[z], rt.at[z], device_id={"width": other}
        )
        share.start()
        own = dot(y, woutv[0])
        out[z] = own.astype(BF16)
        shares.append(share)

    for z in range(batch):
        all_of(send2, recv2, s2, r2, z).wait_send()
    for share in shares:
        share.wait()


def finish(own, theirs, out, total, sem):
    writes = []
    for z in range(own.shape[0]):
        total[z] = (own[z].astype(F32) + theirs[z].astype(F32)).astype(BF16)
        write = pltpu.make_async_copy(total.at[z], out.at[z], sem.at[z])
        write.start()
        writes.append(write)
    for write in writes:
        write.wait()


def shards(tokens, w_in, conv_taps, left_in, right_in, kernel, right_out, left_out, w_out):
    batch, here, half = tokens.shape
    width = w_in.shape[0]
    seq = lax.axis_size("seq")
    lanes = half // 128
    rows = here + 2 * EDGE
    any_space = pl.BlockSpec(memory_space=pltpu.HBM)
    dma, regular = pltpu.SemaphoreType.DMA, pltpu.SemaphoreType.REGULAR
    exchange = pltpu.VMEM((batch, lanes, seq, 2, 128), BF16)
    args = (tokens, w_in.transpose(1, 0, 2), conv_taps, left_in, right_in[0], kernel[0], right_out[0], left_out, w_out)
    args = tuple(pltpu.with_memory_space_constraint(a, pltpu.HBM) for a in args)
    own, theirs = pl.pallas_call(
        layer,
        out_shape=[jax.ShapeDtypeStruct((batch, here, half), BF16)] * 2,
        in_specs=[any_space] * len(args),
        out_specs=[pl.BlockSpec(memory_space=pltpu.VMEM)] * 2,
        scratch_shapes=[
            pltpu.VMEM((batch, rows, width), BF16),
            pltpu.VMEM((3, width, half), BF16),
            pltpu.VMEM(conv_taps.shape, F32),
            pltpu.VMEM(left_in.shape, BF16),
            pltpu.VMEM(right_in.shape[1:], BF16),
            pltpu.VMEM(kernel.shape[1:], BF16),
            pltpu.VMEM(right_out.shape[1:], BF16),
            pltpu.VMEM(left_out.shape, BF16),
            pltpu.VMEM((2, half, half), BF16),
            pltpu.VMEM((batch, 3, here, half), F32),
            pltpu.VMEM((3, 2 * EDGE * batch, half), F32),
            pltpu.VMEM((batch, 3, here + 2 * PAD, half), F32),
            pltpu.VMEM((batch, here, half), F32),
            pltpu.VMEM((here, here), BF16),
            pltpu.VMEM((here, here), BF16),
            exchange, exchange, exchange, exchange,
            pltpu.VMEM((batch, here, half), BF16),
            dma((11,)), dma((5,)), dma((5,)), regular,
            dma((batch,)), dma((batch,)), dma((batch,)), dma((batch,)),
            dma((batch,)), dma((batch,)),
        ],
        compiler_params=pltpu.CompilerParams(collective_id=0, has_side_effects=True, vmem_limit_bytes=24 * 1024 * 1024),
        name="monarch_layer",
    )(*args)
    return pl.pallas_call(
        finish,
        out_shape=jax.ShapeDtypeStruct((batch, here, half), BF16),
        in_specs=[pl.BlockSpec(memory_space=pltpu.VMEM)] * 2,
        out_specs=any_space,
        scratch_shapes=[pltpu.VMEM((batch, here, half), BF16), dma((batch,))],
        compiler_params=pltpu.CompilerParams(vmem_limit_bytes=4 * 1024 * 1024),
        name="final_sum",
    )(own, theirs)


def solution(mesh):
    in_specs = (
        P(None, "seq", "width"),
        P(None, None, "width"),
        P(None, None, "width"),
        P("seq", None, None),
        P("seq", None, None),
        P("seq", None, "width"),
        P("seq", None, None),
        P("seq", None, None),
        P("width", None),
    )
    out_specs = P(None, "seq", "width")
    return jax.shard_map(shards, mesh=mesh, in_specs=in_specs, out_specs=out_specs, check_vma=False)
```

```python
import jax
import jax.numpy as jnp
from jax import lax
from jax.experimental import pallas as pl
from jax.experimental.pallas import tpu as pltpu
from jax.sharding import PartitionSpec as P

BF16 = jnp.bfloat16
F32 = jnp.float32
EDGE = 16
PAD = 8
FIRST = 256


def dot(a, b):
    return jnp.dot(a, b, preferred_element_type=F32)


def spread_rows(count, part):
    rows = lax.broadcasted_iota(jnp.int32, (2 * count, count), 0)
    cols = lax.broadcasted_iota(jnp.int32, (2 * count, count), 1)
    return (rows == 2 * cols + part).astype(BF16)


def spread_cols(count, part):
    rows = lax.broadcasted_iota(jnp.int32, (count, 2 * count), 0)
    cols = lax.broadcasted_iota(jnp.int32, (count, 2 * count), 1)
    return (cols == 2 * rows + part).astype(BF16)


def layer(tok, win, taps, lin, rin, ker, rout, lout, wout, out, recvt,
          tokv, wv, tapv, linv, rinv, kerv, routv, loutv, woutv,
          acc, rim, pad, gate, mix_in, mix_out, send1, recv1, send2, recv2, sendt,
          load_sem, near_send, near_recv, plane_sem, s1, r1, s2, r2, st, rt):
    seq = lax.axis_size("seq")
    me = lax.axis_index("seq")
    w = lax.axis_index("width")
    other = 1 - w
    batch, here, half = tok.shape
    lanes = half // 128
    my, mx, mz = me // 32, (me // 8) % 4, me % 8

    turn = 1 - 2 * w
    ys = [((my + 4 + turn * i) % 4) * 32 for i in range(4)]
    xs = [((mx + 4 + turn * i) % 4) * 8 for i in range(4)]
    zs = [(mz + 8 + turn * i) % 8 for i in range(8)]

    def away(k):
        return ys[k // 32] + xs[(k // 8) % 4] + zs[k % 8]

    right, left = (me + 1) % seq, (me + seq - 1) % seq
    barrier = pltpu.get_barrier_semaphore()
    greet = []
    for s in (right, left):
        greet += [{"seq": s}, {"seq": s, "width": other}]
    greet += [{"seq": away(k)} for k in (4, 3, 5, 2, 6, 1, 7)]
    greet += [{"seq": away(8 * k)} for k in (10, 6, 9, 11, 14, 5, 7, 13, 15, 2, 8, 1, 3, 4, 12)]
    greet += [{"width": other}]
    for who in greet:
        pl.semaphore_signal(barrier, 1, device_id=who)

    own0 = pl.multiple_of(w * half, half)
    sib0 = pl.multiple_of(other * half, half)
    loads = [
        (tok, tokv.at[:, pl.ds(0, here), pl.ds(0, half)]),
        (win.at[:, pl.ds(own0, half)], wv.at[:, pl.ds(0, half)]),
        (win.at[:, pl.ds(sib0, half)], wv.at[:, pl.ds(half, half)]),
        (taps, tapv),
        (lin, linv),
        (rin, rinv),
        (ker, kerv),
        (rout, routv),
        (lout, loutv),
        (wout.at[:, pl.ds(own0, half)], woutv.at[0]),
        (wout.at[:, pl.ds(sib0, half)], woutv.at[1]),
    ]
    loads = [pltpu.make_async_copy(a, b, load_sem.at[i]) for i, (a, b) in enumerate(loads)]
    for load in loads:
        load.start()

    pl.semaphore_wait(barrier, len(greet))
    loads[0].wait()
    near = []
    near.append((tokv.at[:, pl.ds(0, here), pl.ds(0, half)], tokv.at[:, pl.ds(0, here), pl.ds(half, half)], {"width": other}))
    for s, row, to in ((right, here - EDGE, here), (left, 0, here + EDGE)):
        src = tokv.at[:, pl.ds(row, EDGE), pl.ds(0, half)]
        near.append((src, tokv.at[:, pl.ds(to, EDGE), pl.ds(0, half)], {"seq": s}))
        near.append((src, tokv.at[:, pl.ds(to, EDGE), pl.ds(half, half)], {"seq": s, "width": other}))
    near = [
        pltpu.make_async_remote_copy(a, b, near_send.at[i], near_recv.at[i], device_id=who)
        for i, (a, b, who) in enumerate(near)
    ]
    for copy in near[1:] + near[:1]:
        copy.start()
    for k in range(1, 8):
        pl.semaphore_signal(plane_sem, 1, device_id={"seq": away(k)})

    loads[1].wait()
    for z in range(batch):
        for j in range(3):
            acc[z, j] = dot(tokv[z, :here, 0:FIRST], wv[j, 0:FIRST, :])

    loads[4].wait()
    loads[8].wait()
    count = linv.shape[1]
    for a in range(2):
        mix_in[:, count * a : count * (a + 1)] = dot(spread_rows(count, a), linv[a]).astype(BF16)
        mix_out[count * a : count * (a + 1), :] = dot(loutv[a], spread_cols(count, a)).astype(BF16)
    loads[2].wait()
    loads[3].wait()
    def rest(z):
        for j in range(3):
            whole = acc[z, j] + dot(tokv[z, :here, FIRST:], wv[j, FIRST:, :])
            pad[z, j, PAD : PAD + here] = whole.astype(BF16).astype(F32)

    near[0].wait_recv()
    for z in range(batch):
        rest(z)
    for copy in near[1:]:
        copy.wait_recv()
    edges = jnp.concatenate([tokv[z, here:, :] for z in range(batch)], axis=0)
    for j in range(3):
        rim[j] = dot(edges, wv[j]).astype(BF16).astype(F32)

    def hops(k):
        return sum(min(i, n - i) for i, n in ((k // 32, 4), (k // 8 % 4, 4), (k % 8, 8)))

    order = sorted(range(1, seq), key=hops, reverse=True)

    def scatter(src, dst, ssem, rsem, z, early=False):
        head = jnp.where(me == 0, away(order[0]), 0)
        for k in order:
            d = away(k)
            if early:
                d = head if k == order[0] else jnp.where(d == 0, away(order[0]), d)
            pltpu.make_async_remote_copy(
                src.at[z, :, d], dst.at[z, :, me], ssem.at[z], rsem.at[z], device_id={"seq": d}
            ).start()
        dst[z, :, me] = src[z, :, me]

    def all_of(src, dst, ssem, rsem, z):
        rest = pl.ds(0, seq - 1)
        return pltpu.make_async_remote_copy(
            src.at[z, :, rest], dst.at[z, :, rest], ssem.at[z], rsem.at[z], device_id={"seq": me}
        )

    def put(ref, z, value):
        for l in range(lanes):
            ref[z, l] = value[:, 128 * l : 128 * (l + 1)].reshape(seq, 2, 128)

    def take(ref, z):
        return jnp.concatenate([ref[z, l].reshape(2 * seq, 128) for l in range(lanes)], axis=1)

    first, last = me == 0, me == seq - 1
    for z in range(batch):
        conv = []
        for j in range(3):
            low = 2 * EDGE * z + EDGE - 1
            pad[z, j, PAD - 1 : PAD] = jnp.where(first, 0.0, rim[j, low : low + 1])
            pad[z, j, PAD + here : PAD + here + 1] = jnp.where(last, 0.0, rim[j, low + 1 : low + 2])
            conv.append(
                tapv[0, j : j + 1] * pad[z, j, PAD - 1 : PAD - 1 + here]
                + tapv[1, j : j + 1] * pad[z, j, PAD : PAD + here]
                + tapv[2, j : j + 1] * pad[z, j, PAD + 1 : PAD + 1 + here]
            )
            if j == 0:
                gate[z] = conv[0]
        u = (conv[1] * conv[2]).astype(BF16)
        put(send1, z, dot(mix_in[...], u).astype(BF16))
        if z == 0:
            pl.semaphore_wait(plane_sem, 7)
        scatter(send1, recv1, s1, r1, z)

    loads[5].wait()
    loads[6].wait()
    loads[7].wait()
    for z in range(batch):
        all_of(send1, recv1, s1, r1, z).wait_recv()
        second = dot(rinv[...], take(recv1, z))
        freq = (second * kerv[...].astype(F32)).astype(BF16)
        put(send2, z, dot(routv[...], freq).astype(BF16))
        scatter(send2, recv2, s2, r2, z, z == 1)

    loads[9].wait()
    loads[10].wait()
    for copy in near:
        copy.wait_send()
    for z in range(batch):
        all_of(send1, recv1, s1, r1, z).wait_send()
    shares = []
    for z in range(batch):
        all_of(send2, recv2, s2, r2, z).wait_recv()
        fourth = dot(mix_out[...], take(recv2, z))
        y = (gate[z] * fourth).astype(BF16)
        sendt[z] = dot(y, woutv[1]).astype(BF16)
        share = pltpu.make_async_remote_copy(
            sendt.at[z], recvt.at[z], st.at[z], rt.at[z], device_id={"width": other}
        )
        share.start()
        own = dot(y, woutv[0])
        out[z] = own.astype(BF16)
        shares.append(share)

    for z in range(batch):
        all_of(send2, recv2, s2, r2, z).wait_send()
    for share in shares:
        share.wait()


def finish(own, theirs, out, total, sem):
    writes = []
    for z in range(own.shape[0]):
        total[z] = (own[z].astype(F32) + theirs[z].astype(F32)).astype(BF16)
        write = pltpu.make_async_copy(total.at[z], out.at[z], sem.at[z])
        write.start()
        writes.append(write)
    for write in writes:
        write.wait()


def shards(tokens, w_in, conv_taps, left_in, right_in, kernel, right_out, left_out, w_out):
    batch, here, half = tokens.shape
    width = w_in.shape[0]
    seq = lax.axis_size("seq")
    lanes = half // 128
    rows = here + 2 * EDGE
    any_space = pl.BlockSpec(memory_space=pltpu.HBM)
    dma, regular = pltpu.SemaphoreType.DMA, pltpu.SemaphoreType.REGULAR
    exchange = pltpu.VMEM((batch, lanes, seq, 2, 128), BF16)
    args = (tokens, w_in.transpose(1, 0, 2), conv_taps, left_in, right_in[0], kernel[0], right_out[0], left_out, w_out)
    args = tuple(pltpu.with_memory_space_constraint(a, pltpu.HBM) for a in args)
    own, theirs = pl.pallas_call(
        layer,
        out_shape=[jax.ShapeDtypeStruct((batch, here, half), BF16)] * 2,
        in_specs=[any_space] * len(args),
        out_specs=[pl.BlockSpec(memory_space=pltpu.VMEM)] * 2,
        scratch_shapes=[
            pltpu.VMEM((batch, rows, width), BF16),
            pltpu.VMEM((3, width, half), BF16),
            pltpu.VMEM(conv_taps.shape, F32),
            pltpu.VMEM(left_in.shape, BF16),
            pltpu.VMEM(right_in.shape[1:], BF16),
            pltpu.VMEM(kernel.shape[1:], BF16),
            pltpu.VMEM(right_out.shape[1:], BF16),
            pltpu.VMEM(left_out.shape, BF16),
            pltpu.VMEM((2, half, half), BF16),
            pltpu.VMEM((batch, 3, here, half), F32),
            pltpu.VMEM((3, 2 * EDGE * batch, half), F32),
            pltpu.VMEM((batch, 3, here + 2 * PAD, half), F32),
            pltpu.VMEM((batch, here, half), F32),
            pltpu.VMEM((here, here), BF16),
            pltpu.VMEM((here, here), BF16),
            exchange, exchange, exchange, exchange,
            pltpu.VMEM((batch, here, half), BF16),
            dma((11,)), dma((5,)), dma((5,)), regular,
            dma((batch,)), dma((batch,)), dma((batch,)), dma((batch,)),
            dma((batch,)), dma((batch,)),
        ],
        compiler_params=pltpu.CompilerParams(collective_id=0, has_side_effects=True, vmem_limit_bytes=24 * 1024 * 1024),
        name="monarch_layer",
    )(*args)
    return pl.pallas_call(
        finish,
        out_shape=jax.ShapeDtypeStruct((batch, here, half), BF16),
        in_specs=[pl.BlockSpec(memory_space=pltpu.VMEM)] * 2,
        out_specs=any_space,
        scratch_shapes=[pltpu.VMEM((batch, here, half), BF16), dma((batch,))],
        compiler_params=pltpu.CompilerParams(vmem_limit_bytes=4 * 1024 * 1024),
        name="final_sum",
    )(own, theirs)


def solution(mesh):
    in_specs = (
        P(None, "seq", "width"),
        P(None, None, "width"),
        P(None, None, "width"),
        P("seq", None, None),
        P("seq", None, None),
        P("seq", None, "width"),
        P("seq", None, None),
        P("seq", None, None),
        P("width", None),
    )
    out_specs = P(None, "seq", "width")
    return jax.shard_map(shards, mesh=mesh, in_specs=in_specs, out_specs=out_specs, check_vma=False)
```
